32 devices in a mesh: groups: 2 (over y), seq: 4 (over z), pool: 2 (over x), branch: 2 (over core).
Axes of the slice: x: 2, y: 2, z: 4, core: 2. Of those that a mesh axis runs over, the one named last changes fastest.
Arguments:
- video_query: bfloat16 [2, 4096, 3072], P('branch', ('groups', 'seq'), 'pool'), parts along dimension 1, may hold values from -6 to 6
- video_key: bfloat16 [2, 4096, 3072], P('branch', ('groups', 'seq'), 'pool'), parts along dimension 1, may hold values from -6 to 6
- video_value: bfloat16 [2, 4096, 3072], P('branch', ('groups', 'seq'), 'pool'), parts along dimension 1, may hold values from -6 to 6
- cross_query: bfloat16 [2, 4096, 3072], P('branch', ('groups', 'seq'), 'pool'), parts along dimension 1, may hold values from -6 to 6
- audio_key: bfloat16 [2, 512, 3072], P('branch', ('groups', 'seq'), 'pool'), parts along dimension 1, may hold values from -6 to 6
- audio_value: bfloat16 [2, 512, 3072], P('branch', ('groups', 'seq'), 'pool'), parts along dimension 1, may hold values from -6 to 6
- tile_list: int32 [32, 3], P(('groups', 'seq')), parts along dimension 0, may hold values from 0 to 3, as said below
- tile_count: int32 [32], P(('groups', 'seq')), parts along dimension 0, may hold values from 1 to 3
Outputs:
- guided_self: bfloat16 [4096, 3072], P(('groups', 'seq', 'branch'), 'pool'), parts along dimension 0
- guided_cross: bfloat16 [4096, 3072], P(('groups', 'seq', 'branch'), 'pool'), parts along dimension 0
The draws below stay inside these ranges and needn't reach their ends.
There are 2 independent parts, one for each index of `groups`. The reference program is written for one: setup_inputs(seed, part) draws one part's arguments, and reference() takes and returns one part's arrays. A program takes and returns all parts, laid end to end along the dimension named above; each array names one. Nothing has to cross between parts.
Inputs may be any that keep to these rules, and one draw needn't show every extreme that they name: `tile_list`: entry 0 of row v is a = v // 4, the audio tile aligned with video tile v; entries 1 and 2 are a - 1 and a + 1 in an order drawn per row, each clipped to the existing tiles.
All inputs are finite; a program needn't handle non-finite values.
Results may differ from the reference program's by a relative error of at most 0.0051.
Values may be sent and summed in bfloat16 or wider, within the bound.
No kernel may reach another device: no remote copies, remote signals or barrier semaphores. Data moves between devices by JAX's collectives and lax.ppermute only.
A program may use at most 64 MiB of HBM per device.

```python
import jax
import jax.numpy as jnp
from jax import lax

HEADS = 24
DH = 128
VTOK_DEV = 512
VTILE = 128
ATILE = 64
KMAX = 3
FEAT = 3072
VID = 2048
AUD = 256
NVT = 16


def drawn_normal(key, shape):
    return jnp.clip(jax.random.normal(key, shape, jnp.float32), -6.0, 6.0)


def self_pair(key):
    base = jax.random.fold_in(key, 101)
    queries = drawn_normal(jax.random.fold_in(base, 1), (2, VID, FEAT))
    keys = drawn_normal(jax.random.fold_in(base, 2), (2, VID, FEAT))
    return (queries, keys)


def cross_pair(key):
    base = jax.random.fold_in(key, 202)
    queries = drawn_normal(jax.random.fold_in(base, 1), (2, VID, FEAT))
    keys = drawn_normal(jax.random.fold_in(base, 2), (2, AUD, FEAT))
    return (queries, keys)


def offset_values(key, rows, block):
    noise = jax.random.normal(jax.random.fold_in(key, 1), (2, rows // block, block, FEAT), jnp.float32)
    offsets = jax.random.uniform(jax.random.fold_in(key, 2), (2, rows // block, 1, FEAT), jnp.float32, -2.0, 2.0)
    return jnp.clip(0.5 * noise + offsets, -6.0, 6.0).reshape(2, rows, FEAT)


def draw_video_query(key, part):
    return self_pair(key)[0].astype(jnp.bfloat16)


def draw_video_key(key, part):
    return self_pair(key)[1].astype(jnp.bfloat16)


def draw_video_value(key, part):
    return offset_values(jax.random.fold_in(key, 303), VID, VTOK_DEV).astype(jnp.bfloat16)


def draw_cross_query(key, part):
    return cross_pair(key)[0].astype(jnp.bfloat16)


def draw_audio_key(key, part):
    return cross_pair(key)[1].astype(jnp.bfloat16)


def draw_audio_value(key, part):
    return offset_values(jax.random.fold_in(key, 404), AUD, ATILE).astype(jnp.bfloat16)


def draw_tile_list(key, part):
    last_tile = AUD // ATILE - 1
    aligned = jnp.arange(NVT, dtype=jnp.int32) // (VTOK_DEV // VTILE)
    flips = jax.random.randint(jax.random.fold_in(key, 505), (NVT,), 0, 2, dtype=jnp.int32)
    step_one = 2 * flips - 1
    first_side = jnp.clip(aligned + step_one, 0, last_tile)
    second_side = jnp.clip(aligned - step_one, 0, last_tile)
    return jnp.stack([aligned, first_side, second_side], axis=-1).astype(jnp.int32)


def plant(drawn, own_key, smallest, largest):
    longest = drawn.shape.index(max(drawn.shape))
    spots = []
    for shift in (0, 1):
        where = [jax.random.randint(jax.random.fold_in(own_key, axis), (), 0, length) for axis, length in enumerate(drawn.shape)]
        where[longest] = (where[longest] + shift) % drawn.shape[longest]
        spots.append(tuple(where))
    return drawn.at[spots[0]].set(smallest).at[spots[1]].set(largest)


def setup_inputs(seed: int = 0, part: int = 0) -> dict:
    key_of = jax.random.split(jax.random.key(seed), 9)
    own_keys = jax.random.split(jax.random.fold_in(key_of[8], part), 9)
    video_query = draw_video_query(jax.random.fold_in(jax.random.fold_in(key_of[8], part), 71), part)
    video_key = draw_video_key(jax.random.fold_in(jax.random.fold_in(key_of[8], part), 71), part)
    video_value = draw_video_value(jax.random.fold_in(jax.random.fold_in(key_of[8], part), 71), part)
    cross_query = draw_cross_query(jax.random.fold_in(jax.random.fold_in(key_of[8], part), 71), part)
    audio_key = draw_audio_key(jax.random.fold_in(jax.random.fold_in(key_of[8], part), 71), part)
    audio_value = draw_audio_value(jax.random.fold_in(jax.random.fold_in(key_of[8], part), 71), part)
    tile_list = draw_tile_list(jax.random.fold_in(jax.random.fold_in(key_of[8], part), 71), part)
    tile_count = plant(jax.random.randint(own_keys[7], (NVT,), 1, KMAX + 1), jax.random.fold_in(own_keys[7], 1), 1, KMAX).astype(jnp.int32)
    return dict(video_query=video_query, video_key=video_key, video_value=video_value, cross_query=cross_query, audio_key=audio_key, audio_value=audio_value, tile_list=tile_list, tile_count=tile_count)


guidance_weight = 4.0
far_below = -1e30


def attend_block(queries, keys, values, allowed):
    scores = jnp.dot(queries, keys.T, preferred_element_type=jnp.float32) * (DH ** -0.5)
    if allowed is not None:
        scores = jnp.where(allowed, scores, far_below)
    highest = jnp.max(scores, axis=1, keepdims=True)
    expo = jnp.exp(scores - highest)
    numer = jnp.dot(expo.astype(jnp.bfloat16), values, preferred_element_type=jnp.float32)
    denom = jnp.sum(expo, axis=1, keepdims=True)
    return (numer / denom).astype(jnp.bfloat16)


def all_heads(queries, keys, values, allowed):
    blocks = VID // VTOK_DEV

    def per_head(head):
        start = head * DH
        q_head = lax.dynamic_slice_in_dim(queries, start, DH, 1).reshape(blocks, VTOK_DEV, DH)
        k_head = lax.dynamic_slice_in_dim(keys, start, DH, 1)
        v_head = lax.dynamic_slice_in_dim(values, start, DH, 1)
        if allowed is None:
            result = lax.map(lambda block: attend_block(block, k_head, v_head, None), q_head)
        else:
            masks = allowed.reshape(blocks, VTOK_DEV, keys.shape[0])
            result = lax.map(lambda pair: attend_block(pair[0], k_head, v_head, pair[1]), (q_head, masks))
        return result.reshape(VID, DH)

    stacked = lax.map(per_head, jnp.arange(HEADS, dtype=jnp.int32))
    return jnp.transpose(stacked, (1, 0, 2)).reshape(VID, FEAT)


def combine(heads_cond, heads_uncond):
    cond = heads_cond.astype(jnp.float32)
    uncond = heads_uncond.astype(jnp.float32)
    return (uncond + guidance_weight * (cond - uncond)).astype(jnp.bfloat16)


def reference(video_query, video_key, video_value, cross_query, audio_key, audio_value, tile_list, tile_count):
    live = jnp.arange(KMAX, dtype=jnp.int32)[None, :] < tile_count[:, None]
    tiles = jnp.arange(AUD // ATILE, dtype=jnp.int32)
    allowed = jnp.any(live[:, :, None] & (tile_list[:, :, None] == tiles[None, None, :]), axis=1)
    full_mask = jnp.repeat(jnp.repeat(allowed, VTILE, axis=0), ATILE, axis=1)
    self_heads = [all_heads(video_query[b], video_key[b], video_value[b], None) for b in range(2)]
    cross_heads = [all_heads(cross_query[b], audio_key[b], audio_value[b], full_mask) for b in range(2)]
    return combine(self_heads[0], self_heads[1]), combine(cross_heads[0], cross_heads[1])
```

```python
import functools
import math

import jax
import jax.numpy as jnp
from jax import lax
from jax.experimental import pallas as pl
from jax.experimental.pallas import tpu as pltpu
from jax.sharding import PartitionSpec as P

DH = 128
VTILE = 128
ATILE = 64
KMAX = 3

guidance_weight = 4.0
far_below = -1e30
exp2_scale = DH**-0.5 * math.log2(math.e)


def shifted(block, axis, distance):
    count = lax.axis_size(axis)
    return lax.ppermute(block, axis, [(i, (i + distance) % count) for i in range(count)])


def neighbour(block, axis, step):
    count = lax.axis_size(axis)
    route = [(i, i + step) for i in range(count) if 0 <= i + step < count]
    return lax.ppermute(block, axis, route)


def transposed_dot(left, right):
    return lax.dot_general(left, right, (((1,), (1,)), ((), ())), preferred_element_type=jnp.float32)


def pack(where, tensors, head, heads_dest, count):
    rows = tensors[0].shape[1]

    def kernel(where_ref, *refs):
        ins, outs = refs[: 3 * (count - 1)], refs[3 * (count - 1) :]
        for k in range(count - 1):
            for t in range(3):
                outs[k][t] = ins[3 * k + t][0]

    def column(k):
        return lambda i, w: (0, 0, ((w[0] + k) % count) * heads_dest + head)

    return pl.pallas_call(
        kernel,
        grid_spec=pltpu.PrefetchScalarGridSpec(
            num_scalar_prefetch=1,
            grid=(1,),
            in_specs=[
                pl.BlockSpec((1, rows, DH), column(k)) for k in range(1, count) for t in range(3)
            ],
            out_specs=[pl.BlockSpec((3, rows, DH), lambda i, w: (0, 0, 0))] * (count - 1),
        ),
        out_shape=[jax.ShapeDtypeStruct((3, rows, DH), jnp.bfloat16)] * (count - 1),
        cost_estimate=pl.CostEstimate(
            flops=0, bytes_accessed=2 * 3 * (count - 1) * rows * DH * 2, transcendentals=0
        ),
        name="pack",
    )(where, *(tensors * (count - 1)))


def attend(where, tensors, received, head, heads_dest):
    rows = tensors[0].shape[1]
    count = len(received) + 1
    half = rows // 2

    def kernel(where_ref, q_ref, k_ref, v_ref, *refs):
        others, (keep_ref, send_ref, qs, ks, vs) = refs[: count - 1], refs[count - 1 :]
        for scratch, own, t in ((qs, q_ref, 0), (ks, k_ref, 1), (vs, v_ref, 2)):
            scratch[0:rows, :] = own[0]
            for r in range(1, count):
                scratch[r * rows : (r + 1) * rows, :] = others[r - 1][t]
        copy_index = where_ref[1]

        def part(start):
            q = qs[pl.ds(pl.multiple_of(start, half), half), :]
            scores = transposed_dot(q, ks[...])
            highest = jnp.max(scores, axis=1, keepdims=True)
            expo = jnp.exp2((scores - highest) * exp2_scale)
            denom = jnp.sum(expo, axis=1, keepdims=True)
            numer = jnp.dot(expo.astype(jnp.bfloat16), vs[...], preferred_element_type=jnp.float32)
            return (numer / denom).astype(jnp.bfloat16)

        @pl.loop(0, count)
        def _(r):
            keep_ref[r] = part(r * rows + copy_index * half)
            send_ref[r] = part(r * rows + (1 - copy_index) * half)

    tokens = count * rows
    own = pl.BlockSpec((1, rows, DH), lambda i, w: (0, 0, w[0] * heads_dest + head))
    out = pl.BlockSpec((count, half, DH), lambda i, w: (0, 0, 0))
    return pl.pallas_call(
        kernel,
        grid_spec=pltpu.PrefetchScalarGridSpec(
            num_scalar_prefetch=1,
            grid=(1,),
            in_specs=[own] * 3 + [pl.BlockSpec((3, rows, DH), lambda i, w: (0, 0, 0))] * (count - 1),
            out_specs=[out, out],
            scratch_shapes=[pltpu.VMEM((tokens, DH), jnp.bfloat16)] * 3,
        ),
        out_shape=[jax.ShapeDtypeStruct((count, half, DH), jnp.bfloat16)] * 2,
        cost_estimate=pl.CostEstimate(
            flops=4 * tokens * tokens * DH,
            bytes_accessed=4 * tokens * DH * 2,
            transcendentals=tokens * tokens,
        ),
        name="attend",
    )(where, *tensors, *received)


def combine(where, keep, other):
    count, half, width = keep.shape

    def kernel(where_ref, keep_ref, other_ref, *outs):
        first = where_ref[1] == 0
        for r in range(count):
            mine = keep_ref[r].astype(jnp.float32)
            theirs = other_ref[r].astype(jnp.float32)
            cond = jnp.where(first, mine, theirs)
            uncond = jnp.where(first, theirs, mine)
            outs[r][...] = (uncond + guidance_weight * (cond - uncond)).astype(jnp.bfloat16)

    whole = pl.BlockSpec((count, half, width), lambda i, w: (0, 0, 0))
    return pl.pallas_call(
        kernel,
        grid_spec=pltpu.PrefetchScalarGridSpec(
            num_scalar_prefetch=1,
            grid=(1,),
            in_specs=[whole, whole],
            out_specs=[pl.BlockSpec((half, width), lambda i, w: (0, 0))] * count,
        ),
        out_shape=[jax.ShapeDtypeStruct((half, width), jnp.bfloat16)] * count,
        cost_estimate=pl.CostEstimate(
            flops=0, bytes_accessed=3 * count * half * width * 2, transcendentals=0
        ),
        name="combine",
    )(where, keep, other)


def assemble(where, pieces, heads_dest, count):
    half = pieces[0][0].shape[0]
    flat = [piece for head in pieces for piece in head]

    def kernel(where_ref, *refs):
        ins, out = refs[:-1], refs[-1]
        for head in range(heads_dest):
            for r in range(count):
                column = (lax.rem(where_ref[0] + r, count) * heads_dest + head) * DH
                out[:, pl.ds(pl.multiple_of(column, DH), DH)] = ins[head * count + r][...]

    block = pl.BlockSpec((half, DH), lambda i, w: (0, 0))
    width = heads_dest * count * DH
    return pl.pallas_call(
        kernel,
        grid_spec=pltpu.PrefetchScalarGridSpec(
            num_scalar_prefetch=1,
            grid=(1,),
            in_specs=[block] * len(flat),
            out_specs=pl.BlockSpec((half, width), lambda i, w: (0, 0)),
        ),
        out_shape=jax.ShapeDtypeStruct((half, width), jnp.bfloat16),
        cost_estimate=pl.CostEstimate(
            flops=0, bytes_accessed=2 * half * width * 2, transcendentals=0
        ),
        name="assemble",
    )(where, *flat)


def self_by_heads(where, video_query, video_key, video_value):
    count = lax.axis_size("seq")
    heads_dest = video_query.shape[2] // DH // count
    tensors = (video_query, video_key, video_value)
    received = []
    for head in range(heads_dest):
        sent = pack(where, tensors, head, heads_dest, count)
        received.append([shifted(sent[k - 1], "seq", k) for k in range(1, count)])
    pieces = []
    for head in range(heads_dest):
        keep, send = attend(where, tensors, received[head], head, heads_dest)
        other = shifted(send, "branch", 1)
        guided = combine(where, keep, other)
        pieces.append([guided[0]] + [shifted(guided[r], "seq", -r) for r in range(1, count)])
    return assemble(where, pieces, heads_dest, count)


def self_by_rows(video_query, video_key, video_value):
    rows = video_query.shape[1]
    width = video_query.shape[2]
    heads_dev = width // DH
    scale = DH ** (-0.5)
    queries = video_query[0].reshape(rows, heads_dev, DH)
    start_max = jnp.full((heads_dev, rows), far_below, jnp.float32)
    start_total = jnp.zeros((heads_dev, rows), jnp.float32)
    start_accum = jnp.zeros((heads_dev, rows, DH), jnp.float32)
    key_piece = lax.all_gather(video_key[0], "seq", axis=0, tiled=True)
    value_piece = lax.all_gather(video_value[0], "seq", axis=0, tiled=True)
    count = key_piece.shape[0]
    block = math.gcd(count, 512)
    steps = count // block
    key_blocks = key_piece.reshape(steps, block, heads_dev, DH)
    value_blocks = value_piece.reshape(steps, block, heads_dev, DH)

    def one_block(state, pair):
        running_max, total, accum = state
        key_block, value_block = pair
        scores = (
            jnp.einsum("qhd,khd->hqk", queries, key_block, preferred_element_type=jnp.float32)
            * scale
        )
        new_max = jnp.maximum(running_max, jnp.max(scores, axis=-1))
        factor = jnp.exp(running_max - new_max)
        expo = jnp.exp(scores - new_max[:, :, None])
        total = total * factor + jnp.sum(expo, axis=-1)
        accum = accum * factor[:, :, None] + jnp.einsum(
            "hqk,khd->hqd",
            expo.astype(jnp.bfloat16),
            value_block,
            preferred_element_type=jnp.float32,
        )
        return ((new_max, total, accum), None)

    state, unused = lax.scan(
        one_block, (start_max, start_total, start_accum), (key_blocks, value_blocks)
    )
    final_max, total, accum = state
    result = (accum / total[:, :, None]).astype(jnp.bfloat16)
    heads = jnp.transpose(result, (1, 0, 2)).reshape(rows, width)
    half = rows // 2
    copy_index = lax.axis_index("branch")
    keep = lax.dynamic_slice_in_dim(heads, copy_index * half, half, 0)
    send = lax.dynamic_slice_in_dim(heads, (1 - copy_index) * half, half, 0)
    return guide(keep, shifted(send, "branch", 1))


def guide(keep, other):
    is_first = lax.axis_index("branch") == 0
    cond = jnp.where(is_first, keep, other).astype(jnp.float32)
    uncond = jnp.where(is_first, other, keep).astype(jnp.float32)
    return (uncond + guidance_weight * (cond - uncond)).astype(jnp.bfloat16)


def cross(where, cross_query, audio_key, audio_value, tile_list, tile_count):
    rows = cross_query.shape[1]
    width = cross_query.shape[2]
    half = rows // 2
    tiles = rows // VTILE
    sides = [
        (neighbour(a, "seq", 1), a, neighbour(a, "seq", -1)) for a in (audio_key, audio_value)
    ]

    def kernel(where_ref, list_ref, count_ref, q_ref, *refs):
        key_refs, value_refs, (keep_ref, send_ref) = refs[:3], refs[3:6], refs[6:]
        keys = jnp.concatenate([ref[0] for ref in key_refs], axis=0)
        values = jnp.concatenate([ref[0] for ref in value_refs], axis=0)
        tile_of = lax.broadcasted_iota(jnp.int32, (1, 3 * ATILE), 1) // ATILE
        copy_index = where_ref[1]
        per_half = tiles // 2
        for out_ref, first in (
            (keep_ref, copy_index * per_half),
            (send_ref, (1 - copy_index) * per_half),
        ):
            for i in range(per_half):
                v = first + i
                allowed = jnp.zeros((1, 3 * ATILE), jnp.bool_)
                for t in range(3):
                    tile = where_ref[0] + (t - 1)
                    hit = jnp.int32(0)
                    for e in range(KMAX):
                        found = (list_ref[v * KMAX + e] == tile) & (count_ref[v] > e)
                        hit = hit | found.astype(jnp.int32)
                    allowed = allowed | ((tile_of == t) & (hit != 0))
                q = q_ref[0, pl.ds(pl.multiple_of(v * VTILE, VTILE), VTILE), :]
                scores = jnp.where(allowed, transposed_dot(q, keys), far_below)
                highest = jnp.max(scores, axis=1, keepdims=True)
                expo = jnp.exp2((scores - highest) * exp2_scale)
                denom = jnp.sum(expo, axis=1, keepdims=True)
                numer = jnp.dot(
                    expo.astype(jnp.bfloat16), values, preferred_element_type=jnp.float32
                )
                out_ref[i * VTILE : (i + 1) * VTILE, :] = (numer / denom).astype(jnp.bfloat16)

    audio = pl.BlockSpec((1, ATILE, DH), lambda h, *_: (0, 0, h))
    out = pl.BlockSpec((half, DH), lambda h, *_: (0, h))
    keep, send = pl.pallas_call(
        kernel,
        grid_spec=pltpu.PrefetchScalarGridSpec(
            num_scalar_prefetch=3,
            grid=(width // DH,),
            in_specs=[pl.BlockSpec((1, rows, DH), lambda h, *_: (0, 0, h))] + [audio] * 6,
            out_specs=[out, out],
        ),
        out_shape=[jax.ShapeDtypeStruct((half, width), jnp.bfloat16)] * 2,
        cost_estimate=pl.CostEstimate(
            flops=4 * rows * width * 3 * ATILE,
            bytes_accessed=2 * rows * width * 2,
            transcendentals=rows * (width // DH) * 3 * ATILE,
        ),
        name="cross",
    )(where, tile_list.reshape(-1), tile_count, cross_query, *sides[0], *sides[1])
    return guide(keep, shifted(send, "branch", 1))


def shards(
    video_query, video_key, video_value, cross_query, audio_key, audio_value, tile_list, tile_count
):
    where = jnp.stack([lax.axis_index("seq"), lax.axis_index("branch")]).astype(jnp.int32)
    heads_dev = video_query.shape[2] // DH
    guided_cross = cross(where, cross_query, audio_key, audio_value, tile_list, tile_count)
    if heads_dev % lax.axis_size("seq") == 0:
        guided_self = self_by_heads(where, video_query, video_key, video_value)
    else:
        guided_self = self_by_rows(video_query, video_key, video_value)
    return (guided_self, guided_cross)


def solution(mesh):
    placed = (
        P("branch", ("groups", "seq"), "pool"),
        P("branch", ("groups", "seq"), "pool"),
        P("branch", ("groups", "seq"), "pool"),
        P("branch", ("groups", "seq"), "pool"),
        P("branch", ("groups", "seq"), "pool"),
        P("branch", ("groups", "seq"), "pool"),
        P(("groups", "seq"), None),
        P(("groups", "seq")),
    )
    return jax.shard_map(
        shards,
        mesh=mesh,
        in_specs=placed,
        out_specs=(P(("groups", "seq", "branch"), "pool"), P(("groups", "seq", "branch"), "pool")),
        check_vma=False,
    )
```

```python
import math

import jax
import jax.numpy as jnp
from jax import lax
from jax.experimental import pallas as pl
from jax.experimental.pallas import tpu as pltpu
from jax.sharding import PartitionSpec as P


DH = 128
VTILE = 128
ATILE = 64
KMAX = 3

guidance_weight = 4.0
far_below = -1e30
exp2_scale = DH**-0.5 * math.log2(math.e)


def shifted(block, axis, distance):
    count = lax.axis_size(axis)
    return lax.ppermute(block, axis, [(i, (i + distance) % count) for i in range(count)])


def neighbour(block, axis, step):
    count = lax.axis_size(axis)
    route = [(i, i + step) for i in range(count) if 0 <= i + step < count]
    return lax.ppermute(block, axis, route)


def transposed_dot(left, right):
    return lax.dot_general(left, right, (((1,), (1,)), ((), ())), preferred_element_type=jnp.float32)


def pack(where, tensors, head, heads_dest, count):
    rows = tensors[0].shape[1]
    kinds = len(tensors)

    def kernel(where_ref, *refs):
        ins, outs = refs[: kinds * (count - 1)], refs[kinds * (count - 1) :]
        for k in range(count - 1):
            for t in range(kinds):
                outs[k][t] = ins[kinds * k + t][0]

    def column(k):
        return lambda i, w: (0, 0, ((w[0] + k) % count) * heads_dest + head)

    return pl.pallas_call(
        kernel,
        grid_spec=pltpu.PrefetchScalarGridSpec(
            num_scalar_prefetch=1,
            grid=(1,),
            in_specs=[
                pl.BlockSpec((1, rows, DH), column(k))
                for k in range(1, count)
                for _ in range(kinds)
            ],
            out_specs=[pl.BlockSpec((kinds, rows, DH), lambda i, w: (0, 0, 0))] * (count - 1),
        ),
        out_shape=[jax.ShapeDtypeStruct((kinds, rows, DH), jnp.bfloat16)] * (count - 1),
        cost_estimate=pl.CostEstimate(
            flops=0, bytes_accessed=2 * kinds * (count - 1) * rows * DH * 2, transcendentals=0
        ),
        name="pack",
    )(where, *(tuple(tensors) * (count - 1)))


def attend(where, tensors, queries, pairs, head, heads_dest):
    rows = tensors[0].shape[1]
    count = len(pairs) + 1
    half = rows // 2
    shared = queries is pairs
    operands = [*tensors, *pairs] + ([] if shared else queries)

    def kernel(where_ref, q_ref, k_ref, v_ref, *refs):
        pair_refs, refs = refs[: count - 1], refs[count - 1 :]
        query_refs = pair_refs if shared else refs[: count - 1]
        keep_ref, send_ref, qs, ks, vs, sems = refs[-6:]
        column = pl.ds(pl.multiple_of((where_ref[0] * heads_dest + head) * DH, DH), DH)

        def fetch(r, own, other, at, scratch, sem):
            source = other[r - 1].at[at] if r else own.at[0, :, column]
            return pltpu.make_async_copy(source, scratch.at[r * rows : (r + 1) * rows], sem)

        key_copies = [
            fetch(r, k_ref, pair_refs, pairs[0].shape[0] - 2, ks, sems.at[0, r])
            for r in range(count)
        ]
        query_copies = [
            fetch(r, q_ref, query_refs, 0, qs, sems.at[1, r]) for r in range(count)
        ]
        value_copies = [
            fetch(r, v_ref, pair_refs, pairs[0].shape[0] - 1, vs, sems.at[2, r])
            for r in range(count)
        ]
        for copy in key_copies + query_copies + value_copies:
            copy.start()
        for copy in key_copies + query_copies + value_copies:
            copy.wait()
        copy_index = where_ref[1]

        def part(start):
            q = qs[pl.ds(pl.multiple_of(start, half), half), :]
            scores = transposed_dot(q, ks[...])
            highest = jnp.max(scores, axis=1, keepdims=True)
            expo = jnp.exp2((scores - highest) * exp2_scale)
            denom = jnp.sum(expo, axis=1, keepdims=True)
            numer = jnp.dot(expo.astype(jnp.bfloat16), vs[...], preferred_element_type=jnp.float32)
            return (numer / denom).astype(jnp.bfloat16)

        @pl.loop(0, count)
        def _(i):
            keep_ref[i] = part(i * rows + copy_index * half)
            send_ref[i] = part(i * rows + (1 - copy_index) * half)

    tokens = count * rows
    out = pl.BlockSpec((count, half, DH), lambda i, w: (0, 0, 0))
    return pl.pallas_call(
        kernel,
        grid_spec=pltpu.PrefetchScalarGridSpec(
            num_scalar_prefetch=1,
            grid=(1,),
            in_specs=[pl.BlockSpec(memory_space=pl.ANY)] * len(operands),
            out_specs=[out, out],
            scratch_shapes=[pltpu.VMEM((tokens, DH), jnp.bfloat16)] * 3
            + [pltpu.SemaphoreType.DMA((3, count))],
        ),
        out_shape=[jax.ShapeDtypeStruct((count, half, DH), jnp.bfloat16)] * 2,
        cost_estimate=pl.CostEstimate(
            flops=4 * tokens * tokens * DH,
            bytes_accessed=4 * tokens * DH * 2,
            transcendentals=tokens * tokens,
        ),
        name="attend",
    )(where, *operands)


def combine(where, keep, other):
    here, half, width = keep.shape

    def kernel(where_ref, keep_ref, other_ref, *outs):
        first = where_ref[1] == 0
        for i in range(here):
            mine = keep_ref[i].astype(jnp.float32)
            theirs = other_ref[i].astype(jnp.float32)
            cond = jnp.where(first, mine, theirs)
            uncond = jnp.where(first, theirs, mine)
            outs[i][...] = (uncond + guidance_weight * (cond - uncond)).astype(jnp.bfloat16)

    whole = pl.BlockSpec((here, half, width), lambda i, w: (0, 0, 0))
    return pl.pallas_call(
        kernel,
        grid_spec=pltpu.PrefetchScalarGridSpec(
            num_scalar_prefetch=1,
            grid=(1,),
            in_specs=[whole, whole],
            out_specs=[pl.BlockSpec((half, width), lambda i, w: (0, 0))] * here,
        ),
        out_shape=[jax.ShapeDtypeStruct((half, width), jnp.bfloat16)] * here,
        cost_estimate=pl.CostEstimate(
            flops=0, bytes_accessed=3 * here * half * width * 2, transcendentals=0
        ),
        name="combine",
    )(where, keep, other)


def column_of(where_ref, head, r, heads_dest, count):
    column = (lax.rem(where_ref[0] + r, count) * heads_dest + head) * DH
    return pl.ds(pl.multiple_of(column, DH), DH)


def assemble(where, pieces, heads_dest, count):
    places = list(pieces)
    half = pieces[places[0]].shape[0]

    def kernel(where_ref, *refs):
        ins, out = refs[:-1], refs[-1]
        for place, ref in zip(places, ins):
            out[:, column_of(where_ref, *place, heads_dest, count)] = ref[...]

    block = pl.BlockSpec((half, DH), lambda i, w: (0, 0))
    width = heads_dest * count * DH
    return pl.pallas_call(
        kernel,
        grid_spec=pltpu.PrefetchScalarGridSpec(
            num_scalar_prefetch=1,
            grid=(1,),
            in_specs=[block] * len(places),
            out_specs=pl.BlockSpec((half, width), lambda i, w: (0, 0)),
        ),
        out_shape=jax.ShapeDtypeStruct((half, width), jnp.bfloat16),
        cost_estimate=pl.CostEstimate(
            flops=0, bytes_accessed=2 * half * width * 2, transcendentals=0
        ),
        name="assemble",
    )(where, *pieces.values())


def complete(where, partial, pieces, heads_dest, count):
    places = list(pieces)
    half, width = partial.shape

    def kernel(where_ref, partial_ref, *refs):
        ins, out, sems = refs[:-2], refs[-2], refs[-1]
        copies = [
            pltpu.make_async_copy(
                ref, out.at[:, column_of(where_ref, *place, heads_dest, count)], sems.at[i]
            )
            for i, (place, ref) in enumerate(zip(places, ins))
        ]
        for copy in copies:
            copy.start()
        for copy in copies:
            copy.wait()

    return pl.pallas_call(
        kernel,
        grid_spec=pltpu.PrefetchScalarGridSpec(
            num_scalar_prefetch=1,
            grid=(1,),
            in_specs=[pl.BlockSpec(memory_space=pl.ANY)]
            + [pl.BlockSpec((half, DH), lambda i, w: (0, 0))] * len(places),
            out_specs=pl.BlockSpec(memory_space=pl.ANY),
            scratch_shapes=[pltpu.SemaphoreType.DMA((len(places),))],
        ),
        out_shape=jax.ShapeDtypeStruct((half, width), jnp.bfloat16),
        input_output_aliases={1: 0},
        cost_estimate=pl.CostEstimate(
            flops=0, bytes_accessed=2 * half * DH * len(places) * 2, transcendentals=0
        ),
        name="complete",
    )(where, partial, *pieces.values())


def send_order(count):
    return sorted(range(1, count), key=lambda k: -min(k, count - k))


def self_by_heads(where, video_query, video_key, video_value):
    count = lax.axis_size("seq")
    heads_dest = video_query.shape[2] // DH // count
    tensors = (video_query, video_key, video_value)
    order = send_order(count)
    last = heads_dest - 1

    def inflow(kinds, head):
        sent = pack(where, kinds, head, heads_dest, count)
        received = [None] * (count - 1)
        for k in order:
            received[k - 1] = shifted(sent[k - 1], "seq", k)
        return received

    def outflow(queries, pairs, head):
        keep, send = attend(where, tensors, queries, pairs, head, heads_dest)
        other = shifted(send, "branch", 1)
        guided = combine(where, keep, other)
        done = {(head, 0): guided[0]}
        for r in order:
            done[head, r] = shifted(guided[r], "seq", -r)
        return done

    received = [inflow(tensors, head) for head in range(heads_dest)]
    pieces = {}
    for head in range(last):
        pieces |= outflow(received[head], received[head], head)
    final = outflow(received[last], received[last], last)
    pieces[last, 0] = final.pop((last, 0))
    partial = assemble(where, pieces, heads_dest, count)
    return complete(where, partial, final, heads_dest, count)


def self_by_rows(video_query, video_key, video_value):
    rows = video_query.shape[1]
    width = video_query.shape[2]
    heads_dev = width // DH
    scale = DH ** (-0.5)
    queries = video_query[0].reshape(rows, heads_dev, DH)
    start_max = jnp.full((heads_dev, rows), far_below, jnp.float32)
    start_total = jnp.zeros((heads_dev, rows), jnp.float32)
    start_accum = jnp.zeros((heads_dev, rows, DH), jnp.float32)
    key_piece = lax.all_gather(video_key[0], "seq", axis=0, tiled=True)
    value_piece = lax.all_gather(video_value[0], "seq", axis=0, tiled=True)
    count = key_piece.shape[0]
    block = math.gcd(count, 512)
    steps = count // block
    key_blocks = key_piece.reshape(steps, block, heads_dev, DH)
    value_blocks = value_piece.reshape(steps, block, heads_dev, DH)

    def one_block(state, pair):
        running_max, total, accum = state
        key_block, value_block = pair
        scores = (
            jnp.einsum("qhd,khd->hqk", queries, key_block, preferred_element_type=jnp.float32)
            * scale
        )
        new_max = jnp.maximum(running_max, jnp.max(scores, axis=-1))
        factor = jnp.exp(running_max - new_max)
        expo = jnp.exp(scores - new_max[:, :, None])
        total = total * factor + jnp.sum(expo, axis=-1)
        accum = accum * factor[:, :, None] + jnp.einsum(
            "hqk,khd->hqd",
            expo.astype(jnp.bfloat16),
            value_block,
            preferred_element_type=jnp.float32,
        )
        return ((new_max, total, accum), None)

    state, _ = lax.scan(
        one_block, (start_max, start_total, start_accum), (key_blocks, value_blocks)
    )
    _, total, accum = state
    result = (accum / total[:, :, None]).astype(jnp.bfloat16)
    heads = jnp.transpose(result, (1, 0, 2)).reshape(rows, width)
    half = rows // 2
    copy_index = lax.axis_index("branch")
    keep = lax.dynamic_slice_in_dim(heads, copy_index * half, half, 0)
    send = lax.dynamic_slice_in_dim(heads, (1 - copy_index) * half, half, 0)
    return guide(keep, shifted(send, "branch", 1))


def guide(keep, other):
    is_first = lax.axis_index("branch") == 0
    cond = jnp.where(is_first, keep, other).astype(jnp.float32)
    uncond = jnp.where(is_first, other, keep).astype(jnp.float32)
    return (uncond + guidance_weight * (cond - uncond)).astype(jnp.bfloat16)


def cross(where, cross_query, audio_key, audio_value, tile_list, tile_count):
    rows = cross_query.shape[1]
    width = cross_query.shape[2]
    half = rows // 2
    tiles = rows // VTILE
    keys_here = 3 * ATILE
    heads_step = math.gcd(width // DH, 3)
    block = heads_step * DH
    sides = [(neighbour(a, "seq", 1), a, neighbour(a, "seq", -1)) for a in (audio_key, audio_value)]
    tile_ids = where[0] - 1 + jnp.arange(keys_here, dtype=jnp.int32) // ATILE
    live = jnp.arange(KMAX, dtype=jnp.int32)[None, :] < tile_count[:, None]
    allowed = jnp.any(live[:, :, None] & (tile_list[:, :, None] == tile_ids[None, None, :]), axis=1)

    def kernel(where_ref, allowed_ref, q_ref, *refs):
        key_refs, value_refs = refs[:3], refs[3:6]
        keep_ref, send_ref, result = refs[6:]
        mask = jnp.concatenate(
            [
                jnp.broadcast_to(allowed_ref[v : v + 1, :] != 0, (VTILE, keys_here))
                for v in range(tiles)
            ],
            axis=0,
        )
        for h in range(heads_step):
            at = slice(h * DH, (h + 1) * DH)
            keys = jnp.concatenate([ref[0, :, at] for ref in key_refs], axis=0)
            values = jnp.concatenate([ref[0, :, at] for ref in value_refs], axis=0)
            scores = jnp.where(mask, transposed_dot(q_ref[0, :, at], keys), far_below)
            highest = jnp.max(scores, axis=1, keepdims=True)
            expo = jnp.exp2((scores - highest) * exp2_scale)
            denom = jnp.sum(expo, axis=1, keepdims=True)
            numer = jnp.dot(expo.astype(jnp.bfloat16), values, preferred_element_type=jnp.float32)
            result[:, at] = (numer / denom).astype(jnp.bfloat16)
        for ref, which in ((keep_ref, where_ref[1]), (send_ref, 1 - where_ref[1])):
            ref[...] = result[pl.ds(pl.multiple_of(which * half, half), half), :]

    audio = pl.BlockSpec((1, ATILE, block), lambda h, w: (0, 0, h))
    out = pl.BlockSpec((half, block), lambda h, w: (0, h))
    call = pl.pallas_call(
        kernel,
        grid_spec=pltpu.PrefetchScalarGridSpec(
            num_scalar_prefetch=1,
            grid=(width // block,),
            in_specs=[
                pl.BlockSpec((tiles, keys_here), lambda h, w: (0, 0)),
                pl.BlockSpec((1, rows, block), lambda h, w: (0, 0, h)),
                *[audio] * 6,
            ],
            out_specs=[out, out],
            scratch_shapes=[pltpu.VMEM((rows, block), jnp.bfloat16)],
        ),
        out_shape=[jax.ShapeDtypeStruct((half, width), jnp.bfloat16)] * 2,
        cost_estimate=pl.CostEstimate(
            flops=4 * rows * width * keys_here,
            bytes_accessed=2 * rows * width * 2,
            transcendentals=rows * (width // DH) * keys_here,
        ),
        name="cross_kernel",
    )
    keep, send = call(where, allowed.astype(jnp.int32), cross_query, *sides[0], *sides[1])
    other = shifted(send, "branch", 1)
    return guide(keep, other)


def shards(
    video_query, video_key, video_value, cross_query, audio_key, audio_value, tile_list, tile_count
):
    where = jnp.stack([lax.axis_index("seq"), lax.axis_index("branch")]).astype(jnp.int32)
    heads_dev = video_query.shape[2] // DH
    guided_cross = cross(where, cross_query, audio_key, audio_value, tile_list, tile_count)
    if heads_dev % lax.axis_size("seq") == 0:
        guided_self = self_by_heads(where, video_query, video_key, video_value)
    else:
        guided_self = self_by_rows(video_query, video_key, video_value)
    return (guided_self, guided_cross)


def solution(mesh):
    placed = (
        P("branch", ("groups", "seq"), "pool"),
        P("branch", ("groups", "seq"), "pool"),
        P("branch", ("groups", "seq"), "pool"),
        P("branch", ("groups", "seq"), "pool"),
        P("branch", ("groups", "seq"), "pool"),
        P("branch", ("groups", "seq"), "pool"),
        P(("groups", "seq"), None),
        P(("groups", "seq")),
    )
    return jax.shard_map(
        shards,
        mesh=mesh,
        in_specs=placed,
        out_specs=(P(("groups", "seq", "branch"), "pool"), P(("groups", "seq", "branch"), "pool")),
        check_vma=False,
    )
```

```python
import math

import jax
import jax.numpy as jnp
from jax import lax
from jax.experimental import pallas as pl
from jax.experimental.pallas import tpu as pltpu
from jax.sharding import PartitionSpec as P


DH = 128
VTILE = 128
ATILE = 64
KMAX = 3

guidance_weight = 4.0
far_below = -1e30
exp2_scale = DH**-0.5 * math.log2(math.e)


def shifted(block, axis, distance):
    count = lax.axis_size(axis)
    return lax.ppermute(block, axis, [(i, (i + distance) % count) for i in range(count)])


def neighbour(block, axis, step):
    count = lax.axis_size(axis)
    route = [(i, i + step) for i in range(count) if 0 <= i + step < count]
    return lax.ppermute(block, axis, route)


def transposed_dot(left, right):
    return lax.dot_general(left, right, (((1,), (1,)), ((), ())), preferred_element_type=jnp.float32)


def attend(where, tensors, queries, pairs, head, heads_dest):
    rows = tensors[0].shape[1]
    count = len(pairs) + 1
    half = rows // 2
    shared = queries is pairs
    operands = [*tensors, *pairs] + ([] if shared else queries)

    def kernel(where_ref, q_ref, k_ref, v_ref, *refs):
        pair_refs, refs = refs[: count - 1], refs[count - 1 :]
        query_refs = pair_refs if shared else refs[: count - 1]
        keep_ref, send_ref, qs, ks, vs, scores, sems = refs[-7:]
        column = pl.ds(pl.multiple_of((where_ref[0] * heads_dest + head) * DH, DH), DH)

        def fetch(r, own, other, at, scratch, sem):
            source = other[r - 1].at[at] if r else own.at[0, :, column]
            target = scratch.at[r * rows : (r + 1) * rows, 0:DH]
            return pltpu.make_async_copy(source, target, sem)

        key_copies = [
            fetch(r, k_ref, pair_refs, pairs[0].shape[0] - 2, ks, sems.at[0, r])
            for r in range(count)
        ]
        query_copies = [
            fetch(r, q_ref, query_refs, 0, qs, sems.at[1, r]) for r in range(count)
        ]
        value_copies = [
            fetch(r, v_ref, pair_refs, pairs[0].shape[0] - 1, vs, sems.at[2, r])
            for r in range(count)
        ]
        for copy in key_copies + query_copies + value_copies:
            copy.start()
        vs[:, DH:] = jnp.ones((count * rows, DH), jnp.bfloat16)
        copy_index = where_ref[1]

        def score(i, side):
            start = i * rows + lax.rem(copy_index + side, 2) * half
            q = qs[pl.ds(pl.multiple_of(start, half), half), :]
            scores[side] = transposed_dot(q, ks[...])

        def finish(side):
            highest = jnp.max(scores[side], axis=1, keepdims=True)
            expo = jnp.exp2((scores[side] - highest) * exp2_scale)
            sums = jnp.dot(expo.astype(jnp.bfloat16), vs[...], preferred_element_type=jnp.float32)
            return (sums[:, :DH] / sums[:, DH:]).astype(jnp.bfloat16)

        for copy in key_copies + query_copies:
            copy.wait()
        score(0, 0)
        for copy in value_copies:
            copy.wait()

        @pl.loop(0, count)
        def _(i):
            score(i, 1)
            keep_ref[i] = finish(0)
            score(jnp.minimum(i + 1, count - 1), 0)
            send_ref[i] = finish(1)

    tokens = count * rows
    out = pl.BlockSpec((count, half, DH), lambda i, w: (0, 0, 0))
    return pl.pallas_call(
        kernel,
        grid_spec=pltpu.PrefetchScalarGridSpec(
            num_scalar_prefetch=1,
            grid=(1,),
            in_specs=[pl.BlockSpec(memory_space=pl.ANY)] * len(operands),
            out_specs=[out, out],
            scratch_shapes=[pltpu.VMEM((tokens, DH), jnp.bfloat16)] * 2
            + [
                pltpu.VMEM((tokens, 2 * DH), jnp.bfloat16),
                pltpu.VMEM((2, half, tokens), jnp.float32),
                pltpu.SemaphoreType.DMA((3, count)),
            ],
        ),
        out_shape=[jax.ShapeDtypeStruct((count, half, DH), jnp.bfloat16)] * 2,
        cost_estimate=pl.CostEstimate(
            flops=4 * tokens * tokens * DH,
            bytes_accessed=4 * tokens * DH * 2,
            transcendentals=tokens * tokens,
        ),
        name="attend",
    )(where, *operands)


def self_by_heads(where, video_query, video_key, video_value):
    count = lax.axis_size("seq")
    here = lax.axis_index("seq")
    heads_dest = video_query.shape[2] // DH // count
    half = video_query.shape[1] // 2
    tensors = (video_query, video_key, video_value)

    def column(steps, head):
        return ((here + steps) % count * heads_dest + head) * DH

    received = []
    for head in range(heads_dest):
        slots = []
        for k in range(1, count):
            sent = jnp.concatenate(
                [lax.dynamic_slice_in_dim(t, column(k, head), DH, 2) for t in tensors]
            )
            if head == 0 and k == 1:
                sent, *tensors = lax.optimization_barrier((sent, *tensors))
            slots.append(shifted(sent, "seq", k))
        received.append(slots)
    pieces = []
    for heads in (range(heads_dest - 1), [heads_dest - 1]):
        keeps, others = [], []
        for head in heads:
            keep, send = attend(where, tensors, received[head], received[head], head, heads_dest)
            others.append(shifted(send, "branch", 1))
            keeps.append(keep)
        for k in range(count) if heads else ():
            rows = jnp.concatenate(
                [guide(keep[k], other[k]) for keep, other in zip(keeps, others)], axis=1
            )
            if k:
                rows = shifted(rows, "seq", -k)
            pieces.append((k > 0, column(k, heads[0]), rows))
    out = jnp.zeros((half, video_query.shape[2]), jnp.bfloat16)
    out, _ = lax.optimization_barrier((out, others[-1]))
    for remote in (False, True):
        for moved, start, rows in pieces:
            if moved == remote:
                out = lax.dynamic_update_slice_in_dim(out, rows, start, 1)
    return out


def self_by_rows(video_query, video_key, video_value):
    rows = video_query.shape[1]
    width = video_query.shape[2]
    heads_dev = width // DH
    scale = DH ** (-0.5)
    queries = video_query[0].reshape(rows, heads_dev, DH)
    start_max = jnp.full((heads_dev, rows), far_below, jnp.float32)
    start_total = jnp.zeros((heads_dev, rows), jnp.float32)
    start_accum = jnp.zeros((heads_dev, rows, DH), jnp.float32)
    key_piece = lax.all_gather(video_key[0], "seq", axis=0, tiled=True)
    value_piece = lax.all_gather(video_value[0], "seq", axis=0, tiled=True)
    count = key_piece.shape[0]
    block = math.gcd(count, 512)
    steps = count // block
    key_blocks = key_piece.reshape(steps, block, heads_dev, DH)
    value_blocks = value_piece.reshape(steps, block, heads_dev, DH)

    def one_block(state, pair):
        running_max, total, accum = state
        key_block, value_block = pair
        scores = (
            jnp.einsum("qhd,khd->hqk", queries, key_block, preferred_element_type=jnp.float32)
            * scale
        )
        new_max = jnp.maximum(running_max, jnp.max(scores, axis=-1))
        factor = jnp.exp(running_max - new_max)
        expo = jnp.exp(scores - new_max[:, :, None])
        total = total * factor + jnp.sum(expo, axis=-1)
        accum = accum * factor[:, :, None] + jnp.einsum(
            "hqk,khd->hqd",
            expo.astype(jnp.bfloat16),
            value_block,
            preferred_element_type=jnp.float32,
        )
        return ((new_max, total, accum), None)

    state, _ = lax.scan(
        one_block, (start_max, start_total, start_accum), (key_blocks, value_blocks)
    )
    _, total, accum = state
    result = (accum / total[:, :, None]).astype(jnp.bfloat16)
    heads = jnp.transpose(result, (1, 0, 2)).reshape(rows, width)
    half = rows // 2
    copy_index = lax.axis_index("branch")
    keep = lax.dynamic_slice_in_dim(heads, copy_index * half, half, 0)
    send = lax.dynamic_slice_in_dim(heads, (1 - copy_index) * half, half, 0)
    return guide(keep, shifted(send, "branch", 1))


def guide(keep, other):
    is_first = lax.axis_index("branch") == 0
    cond = jnp.where(is_first, keep, other).astype(jnp.float32)
    uncond = jnp.where(is_first, other, keep).astype(jnp.float32)
    return (uncond + guidance_weight * (cond - uncond)).astype(jnp.bfloat16)


def cross(where, cross_query, audio_key, audio_value, tile_list, tile_count):
    rows = cross_query.shape[1]
    width = cross_query.shape[2]
    half = rows // 2
    tiles = rows // VTILE
    keys_here = 3 * ATILE
    heads_step = math.gcd(width // DH, 3)
    block = heads_step * DH
    sides = [(neighbour(a, "seq", 1), a, neighbour(a, "seq", -1)) for a in (audio_key, audio_value)]
    tile_ids = where[0] - 1 + jnp.arange(keys_here, dtype=jnp.int32) // ATILE
    live = jnp.arange(KMAX, dtype=jnp.int32)[None, :] < tile_count[:, None]
    allowed = jnp.any(live[:, :, None] & (tile_list[:, :, None] == tile_ids[None, None, :]), axis=1)

    def kernel(where_ref, allowed_ref, q_ref, *refs):
        key_refs, value_refs = refs[:3], refs[3:6]
        keep_ref, send_ref, result = refs[6:]
        mask = jnp.concatenate(
            [
                jnp.broadcast_to(allowed_ref[v : v + 1, :] != 0, (VTILE, keys_here))
                for v in range(tiles)
            ],
            axis=0,
        )
        for h in range(heads_step):
            at = slice(h * DH, (h + 1) * DH)
            keys = jnp.concatenate([ref[0, :, at] for ref in key_refs], axis=0)
            values = jnp.concatenate([ref[0, :, at] for ref in value_refs], axis=0)
            scores = jnp.where(mask, transposed_dot(q_ref[0, :, at], keys), far_below)
            highest = jnp.max(scores, axis=1, keepdims=True)
            expo = jnp.exp2((scores - highest) * exp2_scale)
            denom = jnp.sum(expo, axis=1, keepdims=True)
            numer = jnp.dot(expo.astype(jnp.bfloat16), values, preferred_element_type=jnp.float32)
            result[:, at] = (numer / denom).astype(jnp.bfloat16)
        for ref, which in ((keep_ref, where_ref[1]), (send_ref, 1 - where_ref[1])):
            ref[...] = result[pl.ds(pl.multiple_of(which * half, half), half), :]

    audio = pl.BlockSpec((1, ATILE, block), lambda h, w: (0, 0, h))
    out = pl.BlockSpec((half, block), lambda h, w: (0, h))
    call = pl.pallas_call(
        kernel,
        grid_spec=pltpu.PrefetchScalarGridSpec(
            num_scalar_prefetch=1,
            grid=(width // block,),
            in_specs=[
                pl.BlockSpec((tiles, keys_here), lambda h, w: (0, 0)),
                pl.BlockSpec((1, rows, block), lambda h, w: (0, 0, h)),
                *[audio] * 6,
            ],
            out_specs=[out, out],
            scratch_shapes=[pltpu.VMEM((rows, block), jnp.bfloat16)],
        ),
        out_shape=[jax.ShapeDtypeStruct((half, width), jnp.bfloat16)] * 2,
        cost_estimate=pl.CostEstimate(
            flops=4 * rows * width * keys_here,
            bytes_accessed=2 * rows * width * 2,
            transcendentals=rows * (width // DH) * keys_here,
        ),
        name="cross_kernel",
    )
    keep, send = call(where, allowed.astype(jnp.int32), cross_query, *sides[0], *sides[1])
    other = shifted(send, "branch", 1)
    return guide(keep, other)


def shards(
    video_query, video_key, video_value, cross_query, audio_key, audio_value, tile_list, tile_count
):
    where = jnp.stack([lax.axis_index("seq"), lax.axis_index("branch")]).astype(jnp.int32)
    heads_dev = video_query.shape[2] // DH
    guided_cross = cross(where, cross_query, audio_key, audio_value, tile_list, tile_count)
    count = lax.axis_size("seq")
    if heads_dev % count == 0:
        guided_self = self_by_heads(where, video_query, video_key, video_value)
    else:
        guided_self = self_by_rows(video_query, video_key, video_value)
    return (guided_self, guided_cross)


def solution(mesh):
    placed = (
        P("branch", ("groups", "seq"), "pool"),
        P("branch", ("groups", "seq"), "pool"),
        P("branch", ("groups", "seq"), "pool"),
        P("branch", ("groups", "seq"), "pool"),
        P("branch", ("groups", "seq"), "pool"),
        P("branch", ("groups", "seq"), "pool"),
        P(("groups", "seq"), None),
        P(("groups", "seq")),
    )
    return jax.shard_map(
        shards,
        mesh=mesh,
        in_specs=placed,
        out_specs=(P(("groups", "seq", "branch"), "pool"), P(("groups", "seq", "branch"), "pool")),
        check_vma=False,
    )
```
